32 devices in a mesh: grp: 2 (over x), ctx: 16 (over z, y, core).
Axes of the slice: x: 2, y: 2, z: 4, core: 2. Of those that a mesh axis runs over, the one named last changes fastest.
Arguments:
- queries: bfloat16 [8192, 8192], P(('grp', 'ctx')), parts along dimension 0, may hold values from -14 to 14
- keys: bfloat16 [8192, 1024], P(('grp', 'ctx')), parts along dimension 0, may hold values from -14 to 14
- values: bfloat16 [8192, 1024], P(('grp', 'ctx')), parts along dimension 0, may hold values from -6 to 6
- lengths: int32 [32], P(('grp', 'ctx')), parts along dimension 0, may hold values from 64 to 256, as said below
Outputs:
- attended: bfloat16 [8192, 8192], P(('grp', 'ctx')), parts along dimension 0
The draws below stay inside these ranges and needn't reach their ends.
There are 2 independent parts, one for each index of `grp`. The reference program is written for one: setup_inputs(seed, part) draws one part's arguments, and reference() takes and returns one part's arrays. A program takes and returns all parts, laid end to end along the dimension named above; each array names one. Nothing has to cross between parts.
Inputs may be any that keep to these rules, and one draw needn't show every extreme that they name: `lengths`: block 0 is always full (256 valid tokens).
All inputs are finite; a program needn't handle non-finite values.
Results may differ from the reference program's by a relative error of at most 0.006.
Values may be sent and summed in bfloat16 or wider, within the bound.
No kernel may reach another device: no remote copies, remote signals or barrier semaphores. Data moves between devices by JAX's collectives and lax.ppermute only.
A program may use at most 128 MiB of HBM per device.

```python
import math
import jax
import jax.numpy as jnp
from jax import lax

H = 64
KVH = 8
HD = 128
TOK_DEV = 256
ANCHOR = 256
TOKENS = 4096


def draw_queries(key, part):
    own_key = jax.random.fold_in(key, 11)
    row_width = H * HD
    result_values = jnp.clip(jax.random.normal(own_key, (TOKENS, row_width), jnp.float32), -6.0, 6.0)
    return result_values.astype(jnp.bfloat16)


def draw_keys(key, part):
    own_key = jax.random.fold_in(key, 13)
    row_width = KVH * HD
    result_values = jnp.clip(jax.random.normal(own_key, (TOKENS, row_width), jnp.float32), -6.0, 6.0)
    return result_values.astype(jnp.bfloat16)


def draw_lengths(key, part):
    block_count = TOKENS // TOK_DEV
    drawn_lengths = jax.random.randint(jax.random.fold_in(key, 23), (block_count,), TOK_DEV // 4, TOK_DEV + 1)
    return drawn_lengths.at[0].set(TOK_DEV).astype(jnp.int32)


def levels(key, shape, split, smallest, top_value):
    factor_of, own = 1.0, jax.random.fold_in(key, 6)
    for dim, parts in split:
        steps = jnp.exp(jax.random.uniform(jax.random.fold_in(own, dim), (parts,), jnp.float32, smallest / len(split), top_value / len(split)))
        factor_of = factor_of * jnp.repeat(steps, shape[dim] // parts).reshape([-1 if axis == dim else 1 for axis in range(len(shape))])
    return factor_of


def normal_values(key, shape, spread, limit, split=(), kind=jnp.bfloat16):
    values = jax.random.normal(key, shape, jnp.float32) * spread
    if len(split) > 0:
        values = levels(key, shape, split, -0.22, 0.18) * values
    return jnp.clip(values, min=-limit, max=limit).astype(kind)


def setup_inputs(seed: int = 0, part: int = 0) -> dict:
    seeds = jax.random.split(jax.random.key(seed), 5)
    own_keys = jax.random.split(jax.random.fold_in(seeds[4], part), 5)
    return {
        "queries": draw_queries(jax.random.fold_in(jax.random.fold_in(seeds[4], part), 71), part),
        "keys": draw_keys(jax.random.fold_in(jax.random.fold_in(seeds[4], part), 71), part),
        "values": normal_values(own_keys[2], (TOKENS, KVH * HD), 1.0, 6.0, ((0, 16),)),
        "lengths": draw_lengths(jax.random.fold_in(jax.random.fold_in(seeds[4], part), 71), part),
    }


rope_base = 500000.0
old_context = 8192.0
scale_factor = 8.0
low_factor = 1.0
high_factor = 4.0
masked_score = -1.0e30


def frequencies(head_dim):
    half_size = head_dim // 2
    inverse = rope_base ** (-2.0 * jnp.arange(half_size, dtype=jnp.float32) / head_dim)
    wave_length = 2.0 * math.pi / inverse
    smooth = (old_context / wave_length - low_factor) / (high_factor - low_factor)
    middle = (1.0 - smooth) * inverse / scale_factor + smooth * inverse
    scaled = jnp.where(wave_length > old_context / low_factor, inverse / scale_factor, inverse)
    inside = (wave_length >= old_context / high_factor) & (wave_length <= old_context / low_factor)
    return jnp.where(inside, middle, scaled)


def rotate(tensor, position):
    head_dim = tensor.shape[-1]
    half_size = head_dim // 2
    angles = position.astype(jnp.float32)[:, None] * frequencies(head_dim)[None, :]
    cosine = jnp.cos(angles)[:, None, :]
    sine_part = jnp.sin(angles)[:, None, :]
    widened = tensor.astype(jnp.float32)
    front_half = widened[..., :half_size]
    back_half = widened[..., half_size:]
    turned = jnp.concatenate([front_half * cosine - back_half * sine_part, back_half * cosine + front_half * sine_part], axis=-1)
    return turned.astype(jnp.bfloat16)


def key_mask(row_count, anchor_rows, length, anchor_live):
    query_index = jnp.arange(row_count, dtype=jnp.int32)[:, None]
    column = jnp.arange(anchor_rows + row_count, dtype=jnp.int32)[None, :]
    local_index = column - anchor_rows
    nearby = (local_index <= query_index) & (local_index < length)
    return jnp.where(column < anchor_rows, anchor_live, nearby)


def reference(queries, keys, values, lengths):
    block_count = TOKENS // TOK_DEV
    group_size = H // KVH
    score_scale = HD ** -0.5
    offsets = (jnp.cumsum(lengths) - lengths).astype(jnp.int32)
    anchor_keys = rotate(keys[:ANCHOR].reshape(ANCHOR, KVH, HD), jnp.arange(ANCHOR, dtype=jnp.int32))
    anchor_values = values[:ANCHOR].reshape(ANCHOR, KVH, HD)

    def one_block(inputs):
        query_block, key_block, value_block, length, offset, number = inputs
        position = offset + jnp.arange(TOK_DEV, dtype=jnp.int32)
        roped_queries = rotate(query_block.reshape(TOK_DEV, H, HD), position)
        roped_keys = rotate(key_block.reshape(TOK_DEV, KVH, HD), position)
        joined_keys = jnp.concatenate([anchor_keys, roped_keys], axis=0)
        joined_values = jnp.concatenate([anchor_values, value_block.reshape(TOK_DEV, KVH, HD)], axis=0)
        allowed = key_mask(TOK_DEV, ANCHOR, length, number > 0)
        query_wide = lax.optimization_barrier(roped_queries).astype(jnp.float32).reshape(TOK_DEV, KVH, group_size, HD)
        key_wide = lax.optimization_barrier(joined_keys).astype(jnp.float32)
        scores = jnp.einsum("qgpd,kgd->gpqk", query_wide, key_wide, precision=lax.Precision.HIGHEST) * score_scale
        scores = jnp.where(allowed[None, None], scores, masked_score)
        highest = jnp.max(scores, axis=-1, keepdims=True)
        raised = jnp.exp(scores - highest)
        totals = jnp.sum(raised, axis=-1)
        weights = lax.optimization_barrier(raised.astype(jnp.bfloat16)).astype(jnp.float32)
        mixed_heads = jnp.einsum("gpqk,kgd->gpqd", weights, joined_values.astype(jnp.float32), precision=lax.Precision.HIGHEST)
        mixed_heads = mixed_heads / totals[..., None]
        live_rows = (jnp.arange(TOK_DEV, dtype=jnp.int32) < length)[:, None, None, None]
        output = jnp.where(live_rows, mixed_heads.transpose(2, 0, 1, 3), 0.0)
        return output.reshape(TOK_DEV, H * HD).astype(jnp.bfloat16)

    results = lax.map(one_block, (queries.reshape(block_count, TOK_DEV, H * HD), keys.reshape(block_count, TOK_DEV, KVH * HD), values.reshape(block_count, TOK_DEV, KVH * HD), lengths, offsets, jnp.arange(block_count, dtype=jnp.int32)))
    return results.reshape(TOKENS, H * HD)
```

```python
import functools
import math

import jax
import jax.numpy as jnp
from jax import lax
from jax.experimental import pallas as pl
from jax.experimental.pallas import tpu as pltpu
from jax.sharding import PartitionSpec as P

HD = 128
ANCHOR = 256
NT = (((1,), (1,)), ((), ()))

rope_base = 500000.0
old_context = 8192.0
scale_factor = 8.0
low_factor = 1.0
high_factor = 4.0
masked_score = -1e30


def frequencies(head_dim):
    half_size = head_dim // 2
    inverse = rope_base ** (-2.0 * jnp.arange(half_size, dtype=jnp.float32) / head_dim)
    wave_length = 2.0 * math.pi / inverse
    smooth = (old_context / wave_length - low_factor) / (high_factor - low_factor)
    middle = (1.0 - smooth) * inverse / scale_factor + smooth * inverse
    scaled = jnp.where(wave_length > old_context / low_factor, inverse / scale_factor, inverse)
    inside = (wave_length >= old_context / high_factor) & (wave_length <= old_context / low_factor)
    return jnp.where(inside, middle, scaled)


def tables(position):
    angles = position.astype(jnp.float32)[:, None] * frequencies(HD)[None, :]
    cosine, sine = jnp.cos(angles), jnp.sin(angles)
    return jnp.concatenate([cosine, cosine], 1), jnp.concatenate([-sine, sine], 1)


def halving(count):
    steps, d = [], count // 2
    while d >= 1:
        steps.append([(h, h + d) for h in range(0, count, 2 * d)])
        d //= 2
    return steps


def plan(n):
    depth = n // 4
    tree = halving(depth)
    last = len(tree)
    at = lambda z, y, c: z * 4 + y * 2 + c
    steps = []
    for s in range(last + 2):
        pairs = []
        if s < last:
            pairs += [(at(a, 0, 0), at(b, 0, 0)) for a, b in tree[s]]
        elif s == last:
            pairs += [(at(z, 0, 0), at(z, 1, 0)) for z in range(depth)]
        if s == 0:
            pairs += [(at(0, 0, 1), at(0, 1, 1))]
        elif s <= last:
            pairs += [(at(a, 1, 1), at(b, 1, 1)) for a, b in tree[s - 1]]
        else:
            pairs += [(at(z, 1, 1), at(z, 0, 1)) for z in range(1, depth)]
        steps.append(pairs)
    return steps


def exchange(n, mask):
    return [(i, i ^ mask) for i in range(n)]


def send(x, pairs):
    return lax.ppermute(x, "ctx", pairs)


def spread(chunks_a, chunks_b, n):
    source = lax.axis_index("ctx") == 0
    held = []
    for a, b in zip(chunks_a, chunks_b):
        got = send(jnp.where(source, b, jnp.zeros_like(b)), exchange(n, 1))
        held.append(jnp.where(source, a, got))
    for pairs in plan(n):
        got = [send(x, pairs) for x in held]
        held = [x + g for x, g in zip(held, got)]
    other = [send(x, exchange(n, 1)) for x in held]
    return held, other


def offset_of(length, n):
    me = lax.axis_index("ctx")
    before, total, mask = jnp.zeros_like(length), length, 1
    while mask < n:
        got = send(total, exchange(n, mask))
        before = before + jnp.where((me & mask) > 0, got, 0)
        total = total + got
        mask *= 2
    return before


def rope(x, c, s):
    x = x.astype(jnp.float32)
    return (x * c + pltpu.roll(x, HD // 2, 1) * s).astype(jnp.bfloat16)


def attend(info, q_ref, k_ref, v_ref, ka_ref, va_ref, kb_ref, vb_ref, c_ref, s_ref, ca_ref, sa_ref, *refs, gs, sub):
    o_ref, qs, kc, vc = refs[-4:]
    length, first, mine = info[0], info[1] > 0, info[2] > 0
    rows, anchor = q_ref.shape[0], ka_ref.shape[0]
    half = rows // 2
    c, s = c_ref[...], s_ref[...]
    kr = rope(k_ref[...], c, s)
    ka = jnp.where(mine, ka_ref[...].astype(jnp.float32), kb_ref[...].astype(jnp.float32))
    va = jnp.where(mine, va_ref[...].astype(jnp.float32), vb_ref[...].astype(jnp.float32))
    kar = rope(ka, ca_ref[...], sa_ref[...])
    copy0 = jnp.broadcast_to(kr[:1].astype(jnp.float32), (anchor, HD))
    kc[:anchor, :] = jnp.where(first, copy0, kar.astype(jnp.float32)).astype(jnp.bfloat16)
    kc[anchor:, :] = kr
    live = jnp.where(first, 0.0, 1.0).astype(jnp.float32)
    vc[:anchor, :HD] = jnp.where(first, 0.0, va).astype(jnp.bfloat16)
    vc[:anchor, HD:] = jnp.full((anchor, HD), live, jnp.float32).astype(jnp.bfloat16)
    vc[anchor:, :HD] = v_ref[...]
    vc[anchor:, HD:] = jnp.ones((rows, HD), jnp.bfloat16)
    for r in range(2):
        span = slice(r * half, (r + 1) * half)
        for h in range(gs):
            qs[r, h * half:(h + 1) * half, :] = rope(q_ref[span, h * HD:(h + 1) * HD], c[span], s[span])
    tri = lax.broadcasted_iota(jnp.int32, (half, half), 0) >= lax.broadcasted_iota(jnp.int32, (half, half), 1)
    factor = HD ** -0.5 * math.log2(math.e)
    for r in range(2):
        n = anchor + (r + 1) * half
        span = slice(r * half, (r + 1) * half)
        valid = lax.broadcasted_iota(jnp.int32, (half, HD), 0) + r * half < length
        for h0 in range(0, gs, sub):
            q = qs[r, h0 * half:(h0 + sub) * half, :]
            scores = lax.dot_general(q, kc[:n, :], NT, preferred_element_type=jnp.float32)
            diag = scores[:, n - half:].reshape(sub, half, half)
            diag = jnp.where(tri[None], diag, masked_score).reshape(sub * half, half)
            rest = scores[:, :n - half]
            top = diag
            for t in range(0, n - half, HD):
                top = jnp.maximum(top, rest[:, t:t + HD])
            top = jnp.max(top, axis=1, keepdims=True)
            weights = jnp.concatenate(
                [jnp.exp2((rest - top) * factor).astype(jnp.bfloat16), jnp.exp2((diag - top) * factor).astype(jnp.bfloat16)], axis=1)
            mixed = jnp.dot(weights, vc[:n, :], preferred_element_type=jnp.float32)
            for i in range(sub):
                part = mixed[i * half:(i + 1) * half]
                inv = jnp.where(valid, 1.0 / part[:, HD:], 0.0)
                o_ref[span, (h0 + i) * HD:(h0 + i + 1) * HD] = (part[:, :HD] * inv).astype(jnp.bfloat16)


def attention(info, q, k, v, held, other, own, anchors, old, start, sub=8):
    rows, anchor = q.shape[0], held.shape[0] // 2
    groups = held.shape[1] // HD
    gs = q.shape[1] // k.shape[1]
    col = lambda n, w: pl.BlockSpec((n, w), lambda g, *_: (0, g + start * groups))
    top = pl.BlockSpec((anchor, HD), lambda g, *_: (0, g))
    low = pl.BlockSpec((anchor, HD), lambda g, *_: (1, g))
    full = lambda n: pl.BlockSpec((n, HD), lambda g, *_: (0, 0))
    return pl.pallas_call(
        functools.partial(attend, gs=gs, sub=sub),
        out_shape=jax.ShapeDtypeStruct(q.shape, jnp.bfloat16),
        grid_spec=pltpu.PrefetchScalarGridSpec(
            num_scalar_prefetch=1, grid=(groups,),
            in_specs=[col(rows, gs * HD), col(rows, HD), col(rows, HD), top, low, top, low,
                      full(rows), full(rows), full(anchor), full(anchor)] + [pl.BlockSpec(memory_space=pl.ANY)] * len(old),
            out_specs=col(rows, gs * HD),
            scratch_shapes=[pltpu.VMEM((2, gs * rows // 2, HD), jnp.bfloat16),
                            pltpu.VMEM((anchor + rows, HD), jnp.bfloat16),
                            pltpu.VMEM((anchor + rows, 2 * HD), jnp.bfloat16)]),
        input_output_aliases={12: 0} if old else {},
        compiler_params=pltpu.CompilerParams(vmem_limit_bytes=60 << 20),
        name="attend",
    )(info, q, k, v, held, held, other, other, *own, *anchors, *old)


def body(n, queries, keys, values, lengths):
    rows, width = keys.shape
    streams = 2
    parts = 2 * streams
    w = width // parts
    me = lax.axis_index("ctx")
    own = [jnp.concatenate([keys[:ANCHOR, c * w:(c + 1) * w], values[:ANCHOR, c * w:(c + 1) * w]], 0) for c in range(parts)]
    held, other = spread(own[0::2], own[1::2], n)
    offset = offset_of(lengths, n)
    info = lambda mine: jnp.stack([lengths[0], (me == 0).astype(jnp.int32), mine.astype(jnp.int32)])
    mine_tab = tables(offset + jnp.arange(rows, dtype=jnp.int32))
    anchor_tab = tables(jnp.arange(ANCHOR, dtype=jnp.int32))
    old = ()
    for c in range(parts):
        mine = (me & 1) == (c & 1)
        old = (attention(info(mine), queries, keys, values, held[c // 2], other[c // 2], mine_tab, anchor_tab, old, c),)
    return old[0]


def solution(mesh):
    spec = P(("grp", "ctx"), None)
    return jax.shard_map(
        functools.partial(body, mesh.shape["ctx"]), mesh=mesh,
        in_specs=(spec, spec, spec, P(("grp", "ctx"))), out_specs=spec, check_vma=False)
```
